256 devices in a mesh: lon: 128 (over x, z, y), lat: 2 (over core).
Axes of the slice: x: 4, y: 4, z: 8, core: 2. Of those that a mesh axis runs over, the one named last changes fastest.
Arguments:
- ensemble: float32 [64, 2048, 2048], P(None, 'lon', 'lat'), may hold values from -6 to 6
- obs_lon: int32 [6, 16], replicated, may hold values from 0 to 15
- obs_lat: int32 [6, 16], replicated, may hold values from 0 to 1023
- obs_offset: float32 [6, 2, 16], replicated, may hold values from -0.5 to 0.5
- obs_value: float32 [6, 16], replicated, may hold values from -6 to 6
- obs_error: float32 [6, 16], replicated, may hold values from 0.2 to 2
- owners: int32 [6], replicated, may hold values from 0 to 255
- group_order: int32 [6], replicated, may hold values from 0 to 5, each once
Outputs:
- analysis: float32 [64, 2048, 2048], P(None, 'lon', 'lat')
The draws below stay inside these ranges and needn't reach their ends.
Inputs may be any that keep to these rules, and one draw needn't show every extreme that they name: `owners`: a tile number: longitude tile index times 2 plus latitude tile index. `group_order`: each group once.
All inputs are finite; a program needn't handle non-finite values.
Results may differ from the reference program's by a relative error of at most 0.00024.
Values sent between devices are 32-bit elements; how exact they have to be, the bound alone decides.
No kernel may reach another device: no remote copies, remote signals or barrier semaphores. Data moves between devices by JAX's collectives and lax.ppermute only.
A program may use at most 64 MiB of HBM per device.

```python
import math
import jax
import jax.numpy as jnp
from jax import lax

MEM = 64
CLON = 16
CLAT = 1024
OBS = 16
GROUPS = 6
LAT_TILES = 2
TILES = 256
NLON = 2048
NLAT = 2048


def touch_ends(array, own_key, least, top_value):
    spot = [jax.random.randint(jax.random.fold_in(own_key, axis), (), 0, length) for axis, length in enumerate(array.shape)]
    widest = array.shape.index(max(array.shape))
    beside = spot[:widest] + [(spot[widest] + 1) % array.shape[widest]] + spot[widest + 1:]
    return array.at[tuple(spot)].set(least).at[tuple(beside)].set(top_value)


def shard_levels(key, shape, pieces, low, largest):
    level, own = 1.0, jax.random.fold_in(key, 6)
    for axis_at, blocks in pieces:
        heights = jnp.exp(jax.random.uniform(jax.random.fold_in(own, axis_at), (blocks,), jnp.float32, low / len(pieces), largest / len(pieces)))
        level = level * jnp.repeat(heights, shape[axis_at] // blocks).reshape([-1 if axis == axis_at else 1 for axis in range(len(shape))])
    return level


def gaussian(key, shape, scale, reach, pieces=(), held_as=jnp.bfloat16):
    values = scale * jax.random.normal(key, shape, jnp.float32)
    if pieces:
        values = values * shard_levels(key, shape, pieces, -0.22, 0.18)
    return jnp.clip(values, -reach, reach).astype(held_as)


def setup_inputs(seed: int = 0) -> dict:
    keys = jax.random.split(jax.random.key(seed), 9)
    return {
        "ensemble": gaussian(keys[0], (MEM, NLON, NLAT), 1.0, 6.0, ((1, 128), (2, 2)), jnp.float32),
        "obs_lon": touch_ends(jax.random.randint(keys[1], (GROUPS, OBS), 0, CLON), jax.random.fold_in(keys[1], 1), 0, CLON - 1).astype(jnp.int32),
        "obs_lat": touch_ends(jax.random.randint(keys[2], (GROUPS, OBS), 0, CLAT), jax.random.fold_in(keys[2], 1), 0, CLAT - 1).astype(jnp.int32),
        "obs_offset": jnp.clip(jax.random.uniform(keys[3], (GROUPS, 2, OBS), jnp.float32, -0.5, 0.5), -0.5, 0.5),
        "obs_value": gaussian(keys[4], (GROUPS, OBS), 1.0, 6.0, (), jnp.float32),
        "obs_error": jnp.clip(jnp.exp(jax.random.uniform(keys[5], (GROUPS, OBS), jnp.float32, math.log(0.2), math.log(2.0))), 0.2, 2.0),
        "owners": touch_ends(jax.random.randint(keys[6], (GROUPS,), 0, TILES), jax.random.fold_in(keys[6], 1), 0, TILES - 1).astype(jnp.int32),
        "group_order": jax.random.permutation(keys[7], GROUPS).astype(jnp.int32),
    }


precise = lax.Precision.HIGHEST

def hat_weights(offset):
    return jnp.stack([jnp.maximum(-offset, 0.0), 1.0 - jnp.abs(offset), jnp.maximum(offset, 0.0)])

def serial_update(prior_rows, values, errors):
    members = prior_rows.shape[1]
    scale = jnp.float32(members - 1)

    def one_step(obs_index, carried):
        current_rows, transform = carried
        current = lax.dynamic_index_in_dim(current_rows, obs_index, 0, keepdims=False)
        value = lax.dynamic_index_in_dim(values, obs_index, 0, keepdims=False)
        error = lax.dynamic_index_in_dim(errors, obs_index, 0, keepdims=False)
        mean_row = jnp.mean(current)
        spread = current - mean_row
        variance = jnp.sum(spread * spread) / scale + error
        shrink = 1.0 / (1.0 + jnp.sqrt(error / variance))
        direction = (value - mean_row - shrink * spread) / (scale * variance)
        current_rows = current_rows + jnp.outer(jnp.dot(current_rows, spread, precision=precise), direction)
        transform = transform + jnp.outer(jnp.dot(transform, spread, precision=precise), direction)
        return (current_rows, transform)
    start = (prior_rows, jnp.eye(members, dtype=jnp.float32))
    return lax.fori_loop(0, prior_rows.shape[0], one_step, start)[1]

def stencil_priors(ensemble, lon_cells, lat_cells, offsets):
    lon_hat = hat_weights(offsets[0])
    lat_hat = hat_weights(offsets[1])
    stencil_sum = jnp.zeros((ensemble.shape[0], lon_cells.shape[0]), jnp.float32)
    for lon_step in range(3):
        for lat_step in range(3):
            lon_idx = (lon_cells + (lon_step - 1)).astype(jnp.int32)
            lat_idx = (lat_cells + (lat_step - 1)).astype(jnp.int32)
            inside = ((lon_idx >= 0) & (lon_idx < NLON) & (lat_idx >= 0) & (lat_idx < NLAT)).astype(jnp.float32)
            picked = ensemble[:, jnp.clip(lon_idx, 0, NLON - 1), jnp.clip(lat_idx, 0, NLAT - 1)]
            stencil_sum = stencil_sum + picked * (lon_hat[lon_step] * lat_hat[lat_step] * inside)[None, :]
    return stencil_sum

def reference(ensemble, obs_lon, obs_lat, obs_offset, obs_value, obs_error, owners, group_order):
    total = jnp.eye(MEM, dtype=jnp.float32)
    for position in range(GROUPS):
        group_id = group_order[position]
        owner_tile = owners[group_id]
        lon_cells = (owner_tile // LAT_TILES * CLON + obs_lon[group_id]).astype(jnp.int32)
        lat_cells = (owner_tile % LAT_TILES * CLAT + obs_lat[group_id]).astype(jnp.int32)
        first_rows = stencil_priors(ensemble, lon_cells, lat_cells, obs_offset[group_id])
        prior_rows = jnp.dot(first_rows.T, total, precision=precise)
        group_step = serial_update(prior_rows, obs_value[group_id], obs_error[group_id])
        total = jnp.dot(total, group_step, precision=precise)
    flattened = ensemble.reshape(MEM, -1)
    return jnp.dot(total.T, flattened, precision=precise).reshape(ensemble.shape)
```

```python
import functools

import jax
import jax.numpy as jnp
from jax import lax
from jax.experimental import pallas as pl
from jax.experimental.pallas import tpu as pltpu
from jax.sharding import Mesh
from jax.sharding import PartitionSpec as P

LON = ("lon_0", "lon_1", "lon_2")
LANES = 128
HIGH = lax.Precision.HIGHEST


def priors_kernel(
    sizes, place, lon_in, lat_in, offset_in, value_in, error_in, owners_in, order_in, field,
    rows_t, table, lon, lat, offset, value, error, owners, order, tile, small_sems, sems
):
    groups, obs, members, lon_cells, lat_cells, lat_tiles = sizes
    chunks = lat_cells // LANES
    my_lon, my_lat = place[0], place[1]
    sources = (owners_in, order_in, lon_in, lat_in, offset_in, value_in, error_in)
    targets = (owners, order, lon, lat, offset, value, error)
    small = [
        pltpu.make_async_copy(source, target, small_sems.at[n])
        for n, (source, target) in enumerate(zip(sources, targets))
    ]
    for copy in small:
        copy.start()
    rows_t[...] = jnp.zeros_like(rows_t)
    for copy in small:
        copy.wait()

    def near(turn):
        tile_no = owners[order[turn]]
        lon_gap = tile_no // lat_tiles - my_lon
        lat_gap = tile_no % lat_tiles - my_lat
        return (jnp.abs(lon_gap) <= 1) & (jnp.abs(lat_gap) <= 1)

    touched = near(0)
    for turn in range(1, groups):
        touched = touched | near(turn)

    copies = [
        pltpu.make_async_copy(
            field.at[:, pl.ds(c * LANES, LANES)], tile.at[c], sems.at[c]
        )
        for c in range(chunks)
    ]

    @pl.when(touched)
    def _():
        for copy in copies:
            copy.start()

    lane = lax.broadcasted_iota(jnp.int32, (1, LANES), 1)
    values = jnp.zeros((1, LANES), jnp.float32)
    errors = jnp.zeros((1, LANES), jnp.float32)
    for turn in range(groups):
        group = order[turn]
        for k in range(obs):
            here = lane == turn * obs + k
            values = jnp.where(here, value[group, k], values)
            errors = jnp.where(here, error[group, k], errors)
    sub8 = lax.broadcasted_iota(jnp.int32, (8, LANES), 0)
    table[...] = jnp.where(sub8 == 0, values, errors)

    @pl.when(touched)
    def _():
        for copy in copies:
            copy.wait()

    @pl.loop(0, groups)
    def _(turn):
        @pl.when(near(turn))
        def _():
            group = order[turn]
            tile_no = owners[group]
            lon_base = (tile_no // lat_tiles - my_lon) * lon_cells
            lat_base = (tile_no % lat_tiles - my_lat) * lat_cells

            @pl.loop(0, obs)
            def _(k):
                p = lon_base + lon[group, k]
                q = lat_base + lat[group, k]
                a = offset[group, 0, k]
                b = offset[group, 1, k]
                inside = (p >= -1) & (p <= lon_cells) & (q >= -1) & (q <= lat_cells)

                @pl.when(inside)
                def _():
                    first = jnp.clip(q - 1, 0, lat_cells - 1) // LANES
                    last = jnp.clip(q + 1, 0, lat_cells - 1) // LANES

                    def part(chunk):
                        gap = (lane + chunk * LANES - q).astype(jnp.float32)
                        lat_hat = jnp.maximum(1.0 - jnp.abs(gap - b), 0.0)
                        total = jnp.zeros((members, LANES), jnp.float32)
                        for step in (-1, 0, 1):
                            row = p + step
                            hat = jnp.maximum(1.0 - jnp.abs(step - a), 0.0)
                            hat = jnp.where((row >= 0) & (row < lon_cells), hat, 0.0)
                            row = jnp.clip(row, 0, lon_cells - 1)
                            cells = tile[chunk, pl.ds(row, members, stride=lon_cells), :]
                            total = total + cells * (lat_hat * hat)
                        found = jnp.sum(total, axis=1, keepdims=True)
                        rows_t[...] += jnp.where(lane == turn * obs + k, found, 0.0)

                    part(first)

                    @pl.when(last != first)
                    def _():
                        part(last)


def split(x):
    high = x.astype(jnp.bfloat16)
    return high, (x - high.astype(jnp.float32)).astype(jnp.bfloat16)


def analysis_kernel(
    sizes, rows_t_ref, table, field, out, tile, done, reduced, factors, spreads, in_sems, out_sems
):
    groups, obs, members, lon_cells, lat_cells, lat_tiles = sizes
    count = groups * obs
    chunks = lat_cells // LANES
    reads = [
        pltpu.make_async_copy(field.at[:, pl.ds(c * LANES, LANES)], tile.at[c], in_sems.at[c])
        for c in range(chunks)
    ]
    writes = [
        pltpu.make_async_copy(done.at[c], out.at[:, pl.ds(c * LANES, LANES)], out_sems.at[c])
        for c in range(chunks)
    ]
    for copy in reads:
        copy.start()

    scale = float(members - 1)
    priors = rows_t_ref[...]
    mean = jnp.mean(priors, axis=0, keepdims=True)
    anomalies = priors - mean
    eye = (
        lax.broadcasted_iota(jnp.int32, (members, LANES), 0)
        == lax.broadcasted_iota(jnp.int32, (members, LANES), 1) % members
    ).astype(jnp.float32)
    both = lax.dot_general(
        anomalies,
        jnp.concatenate([anomalies, eye], axis=1),
        (((0,), (0,)), ((), ())),
        precision=HIGH,
        preferred_element_type=jnp.float32,
    )
    innovation = jnp.broadcast_to(table[0:1, :] - mean, (LANES, LANES)).T
    noise_row = table[1:2, :] * scale
    noise = jnp.broadcast_to(noise_row, (LANES, LANES)).T
    square = lax.broadcasted_iota(jnp.int32, (LANES, LANES), 0)
    across = lax.broadcasted_iota(jnp.int32, (LANES, LANES), 1)
    left_all = both[:, :LANES] + jnp.where(square == across, noise_row, 0.0)
    left_all = jnp.where(across == count, innovation, left_all)
    right_all = both[:, LANES:]

    sub = lax.broadcasted_iota(jnp.int32, (obs, LANES), 0)
    half = lax.broadcasted_iota(jnp.int32, (obs, LANES), 1) < members
    for g in range(groups):
        low = g * obs
        left = left_all[low : low + obs]
        right = right_all[low : low + obs]
        if g:
            change = lax.dot_general(
                factors[0:low, :],
                reduced[0:low, :],
                (((0,), (0,)), ((), ())),
                precision=HIGH,
                preferred_element_type=jnp.float32,
            )
            left = left - change[low : low + obs, :LANES]
            right = right - change[low : low + obs, LANES:]
        columns = [
            jnp.broadcast_to(left[:, low + i : low + i + 1], (obs, LANES)) for i in range(obs)
        ]
        inverses = jnp.zeros((obs, LANES), jnp.float32)
        shrinks = jnp.zeros((obs, LANES), jnp.float32)
        for j in range(obs):
            pivot = columns[j][j : j + 1, :]
            inverse = 1.0 / pivot
            shrink = 1.0 / (1.0 + jnp.sqrt(noise[low + j : low + j + 1, :] * inverse))
            inverses = jnp.where(sub == j, inverse, inverses)
            shrinks = jnp.where(sub == j, shrink, shrinks)
            if j == obs - 1:
                break
            factor = jnp.where(sub > j, columns[j] * inverse, 0.0)
            for i in range(j + 1, obs):
                columns[i] = columns[i] - factor * columns[i][j : j + 1, :]
            left = left - factor * left[j : j + 1, :]
            right = right - factor * (right[j : j + 1, :] * jnp.where(half[0:1], 1.0, shrink))
        innovations = jnp.broadcast_to(left[:, count : count + 1], (obs, LANES))
        spreads[low : low + obs, :] = inverses * (innovations - shrinks * right)
        factors[low : low + obs, :] = left * inverses
        reduced[low : low + obs, :LANES] = left
        reduced[low : low + obs, LANES:] = right * jnp.where(half, 1.0, shrinks)

    change = lax.dot_general(
        spreads[...],
        reduced[:, LANES:],
        (((0,), (0,)), ((), ())),
        precision=HIGH,
        preferred_element_type=jnp.float32,
    )[members : 2 * members, :members]
    high, low_part = split(change)
    weights = jnp.concatenate([high, high, low_part], axis=1)

    for c in range(chunks):
        reads[c].wait()

        @pl.loop(0, lon_cells // 4)
        def _(quad):
            cells = [
                tile[c, pl.ds(quad * 4 + r, members, stride=lon_cells), :] for r in range(4)
            ]
            block = jnp.concatenate(cells, axis=1)
            top, rest = split(block)
            new = block + jnp.dot(
                weights,
                jnp.concatenate([top, rest, top], axis=0),
                preferred_element_type=jnp.float32,
            )
            for r in range(4):
                done[c, pl.ds(quad * 4 + r, members, stride=lon_cells), :] = new[
                    :, r * LANES : (r + 1) * LANES
                ]

        writes[c].start()
    for copy in writes:
        copy.wait()


def shifted_sum(shard, axis, steps):
    size = lax.axis_size(axis)
    arrived = [
        lax.ppermute(shard, axis, [(i, (i + step) % size) for i in range(size)]) for step in steps
    ]
    for piece in arrived:
        shard = shard + piece
    return shard


def total_over_tiles(shard):
    shard = shifted_sum(shard, "lat", (1,))
    shard = shifted_sum(shard, "lon_0", (1, 2, 3))
    shard = shifted_sum(shard, "lon_2", (1, 2, 3))
    shard = shifted_sum(shard, "lon_1", (2, 4, 6))
    size = lax.axis_size("lon_1")
    return shard + lax.ppermute(shard, "lon_1", [(i, i ^ 1) for i in range(size)])


def body(ensemble, obs_lon, obs_lat, obs_offset, obs_value, obs_error, owners, group_order):
    members, lon_cells, lat_cells = ensemble.shape
    groups, obs = obs_lon.shape
    sizes = (groups, obs, members, lon_cells, lat_cells, lax.axis_size("lat"))
    chunks = lat_cells // LANES
    flat = ensemble.reshape(members * lon_cells, lat_cells)
    place = jnp.stack([lax.axis_index(LON), lax.axis_index("lat")]).astype(jnp.int32)
    smem = pl.BlockSpec(memory_space=pltpu.SMEM)
    vmem = pl.BlockSpec(memory_space=pltpu.VMEM)
    hbm = pl.BlockSpec(memory_space=pltpu.HBM)
    chunk_shape = (chunks, members * lon_cells, LANES)
    rows_t, table = pl.pallas_call(
        functools.partial(priors_kernel, sizes),
        out_shape=(
            jax.ShapeDtypeStruct((members, LANES), jnp.float32),
            jax.ShapeDtypeStruct((8, LANES), jnp.float32),
        ),
        in_specs=[smem] + [hbm] * 8,
        out_specs=(vmem, vmem),
        scratch_shapes=[
            pltpu.SMEM(obs_lon.shape, jnp.int32),
            pltpu.SMEM(obs_lat.shape, jnp.int32),
            pltpu.SMEM(obs_offset.shape, jnp.float32),
            pltpu.SMEM(obs_value.shape, jnp.float32),
            pltpu.SMEM(obs_error.shape, jnp.float32),
            pltpu.SMEM(owners.shape, jnp.int32),
            pltpu.SMEM(group_order.shape, jnp.int32),
            pltpu.VMEM(chunk_shape, jnp.float32),
            pltpu.SemaphoreType.DMA((7,)),
            pltpu.SemaphoreType.DMA((chunks,)),
        ],
        compiler_params=pltpu.CompilerParams(vmem_limit_bytes=16 << 20),
        name="priors",
    )(
        place,
        *(
            pltpu.with_memory_space_constraint(array, pltpu.HBM)
            for array in (
                obs_lon, obs_lat, obs_offset, obs_value, obs_error, owners, group_order, flat
            )
        ),
    )
    rows_t = total_over_tiles(rows_t)
    count = groups * obs
    result = pl.pallas_call(
        functools.partial(analysis_kernel, sizes),
        out_shape=jax.ShapeDtypeStruct(flat.shape, jnp.float32),
        in_specs=[vmem, vmem, hbm],
        out_specs=hbm,
        scratch_shapes=[
            pltpu.VMEM(chunk_shape, jnp.float32),
            pltpu.VMEM(chunk_shape, jnp.float32),
            pltpu.VMEM((count, 2 * LANES), jnp.float32),
            pltpu.VMEM((count, LANES), jnp.float32),
            pltpu.VMEM((count, LANES), jnp.float32),
            pltpu.SemaphoreType.DMA((chunks,)),
            pltpu.SemaphoreType.DMA((chunks,)),
        ],
        compiler_params=pltpu.CompilerParams(vmem_limit_bytes=32 << 20),
        name="analysis",
    )(rows_t, table, flat)
    return result.reshape(ensemble.shape)


def solution(mesh):
    torus = Mesh(
        mesh.devices.reshape(4, 8, 4, mesh.shape["lat"]), ("lon_0", "lon_1", "lon_2", "lat")
    )
    in_specs = (P(None, LON, "lat"), P(), P(), P(), P(), P(), P(), P())
    out_specs = P(None, LON, "lat")
    return jax.shard_map(body, mesh=torus, in_specs=in_specs, out_specs=out_specs, check_vma=False)
```

```python
import functools

import jax
import jax.numpy as jnp
from jax import lax
from jax.experimental import pallas as pl
from jax.experimental.pallas import tpu as pltpu
from jax.sharding import Mesh
from jax.sharding import PartitionSpec as P

LON = ("lon_0", "lon_1", "lon_2")
LANES = 128
HIGH = lax.Precision.HIGHEST


def priors_kernel(
    sizes, place, lon_in, lat_in, offset_in, owners_in, order_in, field,
    rows_t, tile, lon, lat, offset, owners, order, small_sems, sems
):
    groups, obs, members, lon_cells, lat_cells, lat_tiles = sizes
    chunks = lat_cells // LANES
    my_lon, my_lat = place[0], place[1]
    sources = (owners_in, order_in, lon_in, lat_in, offset_in)
    targets = (owners, order, lon, lat, offset)
    small = [
        pltpu.make_async_copy(source, target, small_sems.at[n])
        for n, (source, target) in enumerate(zip(sources, targets))
    ]
    copies = [
        pltpu.make_async_copy(field.at[:, pl.ds(c * LANES, LANES)], tile.at[c], sems.at[c])
        for c in range(chunks)
    ]
    for copy in small + copies:
        copy.start()
    rows_t[...] = jnp.zeros_like(rows_t)
    lane = lax.broadcasted_iota(jnp.int32, (1, LANES), 1)
    for copy in small + copies:
        copy.wait()

    @pl.loop(0, groups)
    def _(turn):
        group = order[turn]
        owner = owners[group]
        lon_gap = owner // lat_tiles - my_lon
        lat_gap = owner % lat_tiles - my_lat

        @pl.when((jnp.abs(lon_gap) <= 1) & (jnp.abs(lat_gap) <= 1))
        def _():
            @pl.loop(0, obs)
            def _(k):
                p = lon_gap * lon_cells + lon[group, k]
                q = lat_gap * lat_cells + lat[group, k]
                a = offset[group, 0, k]
                b = offset[group, 1, k]
                inside = (p >= -1) & (p <= lon_cells) & (q >= -1) & (q <= lat_cells)

                @pl.when(inside)
                def _():
                    first = jnp.clip(q - 1, 0, lat_cells - 1) // LANES
                    last = jnp.clip(q + 1, 0, lat_cells - 1) // LANES

                    def part(chunk):
                        gap = (lane + chunk * LANES - q).astype(jnp.float32)
                        lat_hat = jnp.maximum(1.0 - jnp.abs(gap - b), 0.0)
                        total = jnp.zeros((members, LANES), jnp.float32)
                        for step in (-1, 0, 1):
                            row = p + step
                            hat = jnp.maximum(1.0 - jnp.abs(step - a), 0.0)
                            hat = jnp.where((row >= 0) & (row < lon_cells), hat, 0.0)
                            row = jnp.clip(row, 0, lon_cells - 1)
                            cells = tile[chunk, pl.ds(row, members, stride=lon_cells), :]
                            total = total + cells * (lat_hat * hat)
                        found = jnp.sum(total, axis=1, keepdims=True)
                        rows_t[...] += jnp.where(lane == turn * obs + k, found, 0.0)

                    part(first)

                    @pl.when(last != first)
                    def _():
                        part(last)


def table_kernel(sizes, value_in, error_in, order_in, values, noises, value, error, order, sems):
    groups, obs, members = sizes[:3]
    copies = [
        pltpu.make_async_copy(source, target, sems.at[n])
        for n, (source, target) in enumerate(
            ((value_in, value), (error_in, error), (order_in, order))
        )
    ]
    for copy in copies:
        copy.start()
    for copy in copies:
        copy.wait()
    for turn in range(groups):
        group = order[turn]
        for k in range(obs):
            row = pl.ds(turn * obs + k, 1)
            values[row, :] = jnp.full((1, LANES), value[group, k], jnp.float32)
            noises[row, :] = jnp.full((1, LANES), error[group, k] * (members - 1.0), jnp.float32)


def split(x):
    high = x.astype(jnp.bfloat16)
    return high, (x - high.astype(jnp.float32)).astype(jnp.bfloat16)


def analysis_kernel(
    sizes, rows_t_ref, values, noises, tile, out, done, reduced, factors, spreads, out_sems
):
    groups, obs, members, lon_cells, lat_cells, lat_tiles = sizes
    count = groups * obs
    chunks = lat_cells // LANES
    priors = rows_t_ref[...]
    mean = jnp.mean(priors, axis=0, keepdims=True)
    anomalies = priors - mean
    eye = (
        lax.broadcasted_iota(jnp.int32, (members, LANES), 0)
        == lax.broadcasted_iota(jnp.int32, (members, LANES), 1) % members
    ).astype(jnp.float32)
    both = lax.dot_general(
        anomalies,
        jnp.concatenate([anomalies, eye], axis=1),
        (((0,), (0,)), ((), ())),
        precision=HIGH,
        preferred_element_type=jnp.float32,
    )
    mean_column = jnp.broadcast_to(mean, (LANES, LANES)).T[:count]
    innovation = values[...] - mean_column
    noise = noises[...]
    down = lax.broadcasted_iota(jnp.int32, (count, LANES), 0)
    across = lax.broadcasted_iota(jnp.int32, (count, LANES), 1)
    left_all = both[:count, :LANES] + jnp.where(down == across, noise, 0.0)
    left_all = jnp.where(across == count, innovation, left_all)
    right_all = both[:count, LANES:]

    sub = lax.broadcasted_iota(jnp.int32, (obs, LANES), 0)
    half = lax.broadcasted_iota(jnp.int32, (obs, LANES), 1) < members
    for g in range(groups):
        low = g * obs
        left = left_all[low : low + obs]
        right = right_all[low : low + obs]
        if g:
            change = lax.dot_general(
                factors[0:low, :],
                reduced[0:low, :],
                (((0,), (0,)), ((), ())),
                precision=HIGH,
                preferred_element_type=jnp.float32,
            )
            left = left - change[low : low + obs, :LANES]
            right = right - change[low : low + obs, LANES:]
        columns = [
            jnp.broadcast_to(left[:, low + i : low + i + 1], (obs, LANES)) for i in range(obs)
        ]
        inverses = jnp.zeros((obs, LANES), jnp.float32)
        shrinks = jnp.zeros((obs, LANES), jnp.float32)
        for j in range(obs):
            pivot = columns[j][j : j + 1, :]
            inverse = 1.0 / pivot
            shrink = 1.0 / (1.0 + jnp.sqrt(noise[low + j : low + j + 1, :] * inverse))
            inverses = jnp.where(sub == j, inverse, inverses)
            shrinks = jnp.where(sub == j, shrink, shrinks)
            if j == obs - 1:
                break
            factor = jnp.where(sub > j, columns[j] * inverse, 0.0)
            for i in range(j + 1, obs):
                columns[i] = columns[i] - factor * columns[i][j : j + 1, :]
            left = left - factor * left[j : j + 1, :]
            right = right - factor * (right[j : j + 1, :] * jnp.where(half[0:1], 1.0, shrink))
        innovations = jnp.broadcast_to(left[:, count : count + 1], (obs, LANES))
        spreads[low : low + obs, :] = inverses * (innovations - shrinks * right)
        factors[low : low + obs, :] = left * inverses
        reduced[low : low + obs, :LANES] = left
        reduced[low : low + obs, LANES:] = right * jnp.where(half, 1.0, shrinks)

    change = lax.dot_general(
        spreads[...],
        reduced[:, LANES:],
        (((0,), (0,)), ((), ())),
        precision=HIGH,
        preferred_element_type=jnp.float32,
    )[members : 2 * members, :members]
    high, low_part = split(change)
    weights = jnp.concatenate([high, high, low_part], axis=1)

    @pl.loop(0, chunks)
    def _(c):
        for part in range(lon_cells // 4):
            cells = [
                tile[c, pl.ds(part * 4 + r, members, stride=lon_cells), :] for r in range(4)
            ]
            block = jnp.concatenate(cells, axis=1)
            top, rest = split(block)
            new = block + jnp.dot(
                weights,
                jnp.concatenate([top, rest, top], axis=0),
                preferred_element_type=jnp.float32,
            )
            for r in range(4):
                done[c, pl.ds(part * 4 + r, members, stride=lon_cells), :] = new[
                    :, r * LANES : (r + 1) * LANES
                ]
        start = pl.multiple_of(c * LANES, LANES)
        pltpu.make_async_copy(done.at[c], out.at[:, pl.ds(start, LANES)], out_sems.at[c]).start()

    for c in range(chunks):
        pltpu.make_async_copy(
            done.at[c], out.at[:, pl.ds(c * LANES, LANES)], out_sems.at[c]
        ).wait()


def pairwise_sum(shard, axis, partners):
    size = lax.axis_size(axis)
    arrived = [
        lax.ppermute(shard, axis, [(i, partner(i)) for i in range(size)]) for partner in partners
    ]
    for piece in arrived:
        shard = shard + piece
    return shard


def total_over_tiles(shard):
    quad = (lambda i: i ^ 1, lambda i: i ^ 2, lambda i: i ^ 3)
    shard = pairwise_sum(shard, "lat", (lambda i: i ^ 1,))
    shard = pairwise_sum(shard, "lon_0", quad)
    shard = pairwise_sum(shard, "lon_2", quad)
    shard = pairwise_sum(shard, "lon_1", (lambda i: 7 - i,))
    return pairwise_sum(shard, "lon_1", quad)


def body(ensemble, obs_lon, obs_lat, obs_offset, obs_value, obs_error, owners, group_order):
    members, lon_cells, lat_cells = ensemble.shape
    groups, obs = obs_lon.shape
    sizes = (groups, obs, members, lon_cells, lat_cells, lax.axis_size("lat"))
    chunks = lat_cells // LANES
    count = groups * obs
    flat = ensemble.reshape(members * lon_cells, lat_cells)
    place = jnp.stack([lax.axis_index(LON), lax.axis_index("lat")]).astype(jnp.int32)
    smem = pl.BlockSpec(memory_space=pltpu.SMEM)
    vmem = pl.BlockSpec(memory_space=pltpu.VMEM)
    hbm = pl.BlockSpec(memory_space=pltpu.HBM)
    chunk_shape = (chunks, members * lon_cells, LANES)
    ensemble_flat, lon, lat, offset, value, error, owner, order = (
        pltpu.with_memory_space_constraint(array, pltpu.HBM)
        for array in (
            flat, obs_lon, obs_lat, obs_offset, obs_value, obs_error, owners, group_order
        )
    )
    rows_t, tile = pl.pallas_call(
        functools.partial(priors_kernel, sizes),
        out_shape=(
            jax.ShapeDtypeStruct((members, LANES), jnp.float32),
            jax.ShapeDtypeStruct(chunk_shape, jnp.float32),
        ),
        in_specs=[smem] + [hbm] * 6,
        out_specs=(vmem, vmem),
        scratch_shapes=[
            pltpu.SMEM(obs_lon.shape, jnp.int32),
            pltpu.SMEM(obs_lat.shape, jnp.int32),
            pltpu.SMEM(obs_offset.shape, jnp.float32),
            pltpu.SMEM(owners.shape, jnp.int32),
            pltpu.SMEM(group_order.shape, jnp.int32),
            pltpu.SemaphoreType.DMA((5,)),
            pltpu.SemaphoreType.DMA((chunks,)),
        ],
        compiler_params=pltpu.CompilerParams(vmem_limit_bytes=10 << 20),
        name="priors",
    )(place, lon, lat, offset, owner, order, ensemble_flat)
    values, noises = pl.pallas_call(
        functools.partial(table_kernel, sizes),
        out_shape=(jax.ShapeDtypeStruct((count, LANES), jnp.float32),) * 2,
        in_specs=[hbm] * 3,
        out_specs=(vmem, vmem),
        scratch_shapes=[
            pltpu.SMEM(obs_value.shape, jnp.float32),
            pltpu.SMEM(obs_error.shape, jnp.float32),
            pltpu.SMEM(group_order.shape, jnp.int32),
            pltpu.SemaphoreType.DMA((3,)),
        ],
        compiler_params=pltpu.CompilerParams(vmem_limit_bytes=1 << 20),
        cost_estimate=pl.CostEstimate(flops=1 << 20, bytes_accessed=4 << 20, transcendentals=0),
        name="tables",
    )(value, error, order)
    rows_t = total_over_tiles(rows_t)
    result = pl.pallas_call(
        functools.partial(analysis_kernel, sizes),
        out_shape=jax.ShapeDtypeStruct(flat.shape, jnp.float32),
        in_specs=[vmem] * 4,
        out_specs=hbm,
        scratch_shapes=[
            pltpu.VMEM(chunk_shape, jnp.float32),
            pltpu.VMEM((count, 2 * LANES), jnp.float32),
            pltpu.VMEM((count, LANES), jnp.float32),
            pltpu.VMEM((count, LANES), jnp.float32),
            pltpu.SemaphoreType.DMA((chunks,)),
        ],
        compiler_params=pltpu.CompilerParams(vmem_limit_bytes=16 << 20),
        name="analysis",
    )(rows_t, values, noises, tile)
    return result.reshape(ensemble.shape)


def solution(mesh):
    torus = Mesh(
        mesh.devices.reshape(4, 8, 4, mesh.shape["lat"]), ("lon_0", "lon_1", "lon_2", "lat")
    )
    in_specs = (P(None, LON, "lat"), P(), P(), P(), P(), P(), P(), P())
    out_specs = P(None, LON, "lat")
    return jax.shard_map(body, mesh=torus, in_specs=in_specs, out_specs=out_specs, check_vma=False)
```

```python
import functools

import jax
import jax.numpy as jnp
from jax import lax
from jax.experimental import pallas as pl
from jax.experimental.pallas import tpu as pltpu
from jax.sharding import Mesh
from jax.sharding import PartitionSpec as P

LON = ("lon_0", "lon_1", "lon_2")
LANES = 128
STEP = 4
HIGH = lax.Precision.HIGHEST


def priors_kernel(
    sizes, place, lon_in, lat_in, offset_in, owners_in, order_in, field,
    rows_t, lon, lat, offset, owners, order, tile, small_sems, sems
):
    groups, obs, members, lon_cells, lat_cells, lat_tiles = sizes
    my_lon, my_lat = place[0], place[1]
    sources = (owners_in, order_in, lon_in, lat_in, offset_in)
    targets = (owners, order, lon, lat, offset)
    small = [
        pltpu.make_async_copy(source, target, small_sems.at[n])
        for n, (source, target) in enumerate(zip(sources, targets))
    ]
    copies = [
        pltpu.make_async_copy(field.at[:, row, :], tile.at[row], sems.at[row])
        for row in range(lon_cells)
    ]
    for copy in small:
        copy.start()
    rows_t[...] = jnp.zeros_like(rows_t)
    lane = lax.broadcasted_iota(jnp.int32, (1, LANES), 1)
    for copy in small:
        copy.wait()

    def gaps(group):
        owner = owners[group]
        return owner // lat_tiles - my_lon, owner % lat_tiles - my_lat

    def near(group):
        lon_gap, lat_gap = gaps(group)
        return (jnp.abs(lon_gap) <= 1) & (jnp.abs(lat_gap) <= 1)

    touched = near(0)
    for group in range(1, groups):
        touched = touched | near(group)

    @pl.when(touched)
    def _():
        for copy in copies:
            copy.start()
        for copy in copies:
            copy.wait()

    @pl.loop(0, groups)
    def _(turn):
        group = order[turn]
        lon_gap, lat_gap = gaps(group)

        @pl.when(near(group))
        def _():
            @pl.loop(0, obs)
            def _(k):
                p = lon_gap * lon_cells + lon[group, k]
                q = lat_gap * lat_cells + lat[group, k]
                a = offset[group, 0, k]
                b = offset[group, 1, k]
                inside = (p >= -1) & (p <= lon_cells) & (q >= -1) & (q <= lat_cells)

                @pl.when(inside)
                def _():
                    first = jnp.clip(q - 1, 0, lat_cells - 1) // LANES
                    last = jnp.clip(q + 1, 0, lat_cells - 1) // LANES

                    def share(chunk):
                        gap = (lane + chunk * LANES - q).astype(jnp.float32)
                        lat_hat = jnp.maximum(1.0 - jnp.abs(gap - b), 0.0)
                        start = pl.multiple_of(chunk * LANES, LANES)
                        total = jnp.zeros((members, LANES), jnp.float32)
                        for step in (-1, 0, 1):
                            row = p + step
                            hat = jnp.maximum(1.0 - jnp.abs(step - a), 0.0)
                            hat = jnp.where((row >= 0) & (row < lon_cells), hat, 0.0)
                            row = jnp.clip(row, 0, lon_cells - 1)
                            total = total + tile[row, :, pl.ds(start, LANES)] * (lat_hat * hat)
                        found = jnp.sum(total, axis=1, keepdims=True)
                        rows_t[...] += jnp.where(lane == turn * obs + k, found, 0.0)

                    share(first)

                    @pl.when(last != first)
                    def _():
                        share(last)


def table_kernel(
    sizes, value_in, error_in, order_in, field, values, noises, tile, value, error, order, sems,
    tile_sems
):
    groups, obs, members, lon_cells = sizes[:4]
    reads = [
        pltpu.make_async_copy(field.at[:, row, :], tile.at[row], tile_sems.at[row])
        for row in range(lon_cells)
    ]
    copies = [
        pltpu.make_async_copy(source, target, sems.at[n])
        for n, (source, target) in enumerate(
            ((value_in, value), (error_in, error), (order_in, order))
        )
    ]
    for copy in copies + reads:
        copy.start()
    for copy in copies:
        copy.wait()
    for turn in range(groups):
        group = order[turn]
        for k in range(obs):
            row = pl.ds(turn * obs + k, 1)
            values[row, :] = jnp.full((1, LANES), value[group, k], jnp.float32)
            noises[row, :] = jnp.full((1, LANES), error[group, k] * (members - 1.0), jnp.float32)
    for copy in reads:
        copy.wait()


def split(x):
    high = x.astype(jnp.bfloat16)
    return high, (x - high.astype(jnp.float32)).astype(jnp.bfloat16)


def analysis_kernel(
    sizes, rows_t_ref, values, noises, tile, out, done, reduced, spreads, out_sems
):
    groups, obs, members, lon_cells, lat_cells, lat_tiles = sizes
    count = groups * obs
    priors = rows_t_ref[...]
    mean = jnp.mean(priors, axis=0, keepdims=True)
    anomalies = priors - mean
    eye = (
        lax.broadcasted_iota(jnp.int32, (members, LANES), 0)
        == lax.broadcasted_iota(jnp.int32, (members, LANES), 1) % members
    ).astype(jnp.float32)
    both = lax.dot_general(
        anomalies,
        jnp.concatenate([anomalies, eye], axis=1),
        (((0,), (0,)), ((), ())),
        precision=HIGH,
        preferred_element_type=jnp.float32,
    )
    mean_column = jnp.broadcast_to(mean, (LANES, LANES)).T[:count]
    innovation = values[...] - mean_column
    noise = noises[...]
    down = lax.broadcasted_iota(jnp.int32, (count, LANES), 0)
    across = lax.broadcasted_iota(jnp.int32, (count, LANES), 1)
    left_all = both[:count, :LANES] + jnp.where(down == across, noise, 0.0)
    left_all = jnp.where(across == count, innovation, left_all)
    right_all = both[:count, LANES:]

    own = lax.broadcasted_iota(jnp.int32, (obs, LANES), 0)
    half = lax.broadcasted_iota(jnp.int32, (obs, LANES), 1) < members
    for g in range(groups):
        low = g * obs
        tall = 2 * obs if g < groups - 1 else obs
        left = left_all[:tall]
        right = right_all[:tall]
        sub = lax.broadcasted_iota(jnp.int32, (tall, LANES), 0)
        columns = [
            jnp.broadcast_to(left[:, low + i : low + i + 1], (tall, LANES)) for i in range(obs)
        ]
        inverses = jnp.zeros((obs, LANES), jnp.float32)
        shrinks = jnp.zeros((obs, LANES), jnp.float32)
        for j in range(0, obs, 2):
            first, second = columns[j], columns[j + 1]
            corner, cross, other = first[j : j + 1], first[j + 1 : j + 2], second[j + 1 : j + 2]
            inverse = 1.0 / corner
            inverse_next = corner / (corner * other - cross * cross)
            slope = cross * inverse
            shrink = 1.0 / (1.0 + jnp.sqrt(noise[low + j : low + j + 1] * inverse))
            shrink_next = 1.0 / (1.0 + jnp.sqrt(noise[low + j + 1 : low + j + 2] * inverse_next))
            inverses = jnp.where(own == j, inverse, jnp.where(own == j + 1, inverse_next, inverses))
            shrinks = jnp.where(own == j, shrink, jnp.where(own == j + 1, shrink_next, shrinks))
            below = jnp.where(sub > j, first, 0.0)
            below_next = jnp.where(sub > j + 1, second - first * slope, 0.0)

            def eliminate(block, weight, weight_next):
                top, under = block[j : j + 1], block[j + 1 : j + 2]
                scaled = (under - (slope * weight) * top) * (inverse_next * weight_next)
                return block - (below * (top * (inverse * weight)) + below_next * scaled)

            for i in range(j + 2, obs):
                columns[i] = eliminate(columns[i], 1.0, 1.0)
            left = eliminate(left, 1.0, 1.0)
            right = eliminate(
                right, jnp.where(half[0:1], 1.0, shrink), jnp.where(half[0:1], 1.0, shrink_next)
            )
        following = (left[obs:], right[obs:])
        left, right = left[:obs], right[:obs]
        innovations = jnp.broadcast_to(left[:, count : count + 1], (obs, LANES))
        spreads[low : low + obs, :] = inverses * (innovations - shrinks * right)
        right = right * jnp.where(half, 1.0, shrinks)
        reduced[low : low + obs, :] = right
        if g == groups - 2:
            left_all, right_all = following
        elif g < groups - 2:
            change = jnp.dot(
                (left * inverses).T[low + 2 * obs : count],
                jnp.concatenate([left, right], axis=1),
                precision=HIGH,
                preferred_element_type=jnp.float32,
            )
            left_all = jnp.concatenate(
                [following[0], left_all[2 * obs :] - change[:, :LANES]], axis=0
            )
            right_all = jnp.concatenate(
                [following[1], right_all[2 * obs :] - change[:, LANES:]], axis=0
            )

    change = lax.dot_general(
        spreads[...],
        reduced[...],
        (((0,), (0,)), ((), ())),
        precision=HIGH,
        preferred_element_type=jnp.float32,
    )[members : 2 * members, :members]
    high, low_part = split(change)
    weights = jnp.concatenate([high, high, low_part], axis=1)

    @pl.loop(0, lat_cells // LANES)
    def _(c):
        lanes = pl.ds(pl.multiple_of(c * LANES, LANES), LANES)
        for part in range(lon_cells // STEP):
            rows = range(part * STEP, (part + 1) * STEP)
            block = jnp.concatenate([tile[row, :, lanes] for row in rows], axis=1)
            top, rest = split(block)
            new = block + jnp.dot(
                weights,
                jnp.concatenate([top, rest, top], axis=0),
                preferred_element_type=jnp.float32,
            )
            for n, row in enumerate(rows):
                done[c, pl.ds(row, members, stride=lon_cells), :] = new[
                    :, n * LANES : (n + 1) * LANES
                ]
        pltpu.make_async_copy(done.at[c], out.at[:, lanes], out_sems.at[c]).start()

    for c in range(lat_cells // LANES):
        pltpu.make_async_copy(
            done.at[c], out.at[:, pl.ds(c * LANES, LANES)], out_sems.at[c]
        ).wait()


def pairwise_sum(shard, axis, partners):
    size = lax.axis_size(axis)
    arrived = [
        lax.ppermute(shard, axis, [(i, partner(i)) for i in range(size)]) for partner in partners
    ]
    for piece in arrived:
        shard = shard + piece
    return shard


def total_over_tiles(shard):
    quad = (lambda i: i ^ 1, lambda i: i ^ 2, lambda i: i ^ 3)
    shard = pairwise_sum(shard, "lat", (lambda i: i ^ 1,))
    shard = pairwise_sum(shard, "lon_0", quad)
    shard = pairwise_sum(shard, "lon_2", quad)
    shard = pairwise_sum(shard, "lon_1", (lambda i: 7 - i,))
    return pairwise_sum(shard, "lon_1", quad)


def body(ensemble, obs_lon, obs_lat, obs_offset, obs_value, obs_error, owners, group_order):
    members, lon_cells, lat_cells = ensemble.shape
    groups, obs = obs_lon.shape
    sizes = (groups, obs, members, lon_cells, lat_cells, lax.axis_size("lat"))
    count = groups * obs
    place = jnp.stack([lax.axis_index(LON), lax.axis_index("lat")]).astype(jnp.int32)
    smem = pl.BlockSpec(memory_space=pltpu.SMEM)
    vmem = pl.BlockSpec(memory_space=pltpu.VMEM)
    hbm = pl.BlockSpec(memory_space=pltpu.HBM)
    tile_shape = (lon_cells, members, lat_cells)
    field, lon, lat, offset, value, error, owner, order = (
        pltpu.with_memory_space_constraint(array, pltpu.HBM)
        for array in (
            ensemble, obs_lon, obs_lat, obs_offset, obs_value, obs_error, owners, group_order
        )
    )
    rows_t = pl.pallas_call(
        functools.partial(priors_kernel, sizes),
        out_shape=jax.ShapeDtypeStruct((members, LANES), jnp.float32),
        in_specs=[smem] + [hbm] * 6,
        out_specs=vmem,
        scratch_shapes=[
            pltpu.SMEM(obs_lon.shape, jnp.int32),
            pltpu.SMEM(obs_lat.shape, jnp.int32),
            pltpu.SMEM(obs_offset.shape, jnp.float32),
            pltpu.SMEM(owners.shape, jnp.int32),
            pltpu.SMEM(group_order.shape, jnp.int32),
            pltpu.VMEM(tile_shape, jnp.float32),
            pltpu.SemaphoreType.DMA((5,)),
            pltpu.SemaphoreType.DMA((lon_cells,)),
        ],
        compiler_params=pltpu.CompilerParams(vmem_limit_bytes=10 << 20),
        name="priors",
    )(place, lon, lat, offset, owner, order, field)
    values, noises, tile = pl.pallas_call(
        functools.partial(table_kernel, sizes),
        out_shape=(
            jax.ShapeDtypeStruct((count, LANES), jnp.float32),
            jax.ShapeDtypeStruct((count, LANES), jnp.float32),
            jax.ShapeDtypeStruct(tile_shape, jnp.float32),
        ),
        in_specs=[hbm] * 4,
        out_specs=(vmem,) * 3,
        scratch_shapes=[
            pltpu.SMEM(obs_value.shape, jnp.float32),
            pltpu.SMEM(obs_error.shape, jnp.float32),
            pltpu.SMEM(group_order.shape, jnp.int32),
            pltpu.SemaphoreType.DMA((3,)),
            pltpu.SemaphoreType.DMA((lon_cells,)),
        ],
        compiler_params=pltpu.CompilerParams(vmem_limit_bytes=6 << 20),
        cost_estimate=pl.CostEstimate(flops=1 << 20, bytes_accessed=4 << 20, transcendentals=0),
        name="tables",
    )(value, error, order, field)
    rows_t = total_over_tiles(rows_t)
    return pl.pallas_call(
        functools.partial(analysis_kernel, sizes),
        out_shape=jax.ShapeDtypeStruct((members * lon_cells, lat_cells), jnp.float32),
        in_specs=[vmem] * 4,
        out_specs=hbm,
        scratch_shapes=[
            pltpu.VMEM((lat_cells // LANES, members * lon_cells, LANES), jnp.float32),
            pltpu.VMEM((count, LANES), jnp.float32),
            pltpu.VMEM((count, LANES), jnp.float32),
            pltpu.SemaphoreType.DMA((lat_cells // LANES,)),
        ],
        compiler_params=pltpu.CompilerParams(vmem_limit_bytes=16 << 20),
        name="analysis",
    )(rows_t, values, noises, tile).reshape(ensemble.shape)


def solution(mesh):
    torus = Mesh(
        mesh.devices.reshape(4, 8, 4, mesh.shape["lat"]), ("lon_0", "lon_1", "lon_2", "lat")
    )
    in_specs = (P(None, LON, "lat"), P(), P(), P(), P(), P(), P(), P())
    out_specs = P(None, LON, "lat")
    return jax.shard_map(body, mesh=torus, in_specs=in_specs, out_specs=out_specs, check_vma=False)
```

```python
import functools

import jax
import jax.numpy as jnp
from jax import lax
from jax.experimental import pallas as pl
from jax.experimental.pallas import tpu as pltpu
from jax.sharding import Mesh
from jax.sharding import PartitionSpec as P

LON = ("lon_0", "lon_1", "lon_2")
LANES = 128
STEP = 4
HIGH = lax.Precision.HIGHEST


def priors_kernel(
    sizes, place, lon_in, lat_in, offset_in, owners_in, order_in, field,
    rows_t, tile, lon, lat, offset, owners, order, small_sems, sems
):
    groups, obs, members, lon_cells, lat_cells, lat_tiles = sizes
    my_lon, my_lat = place[0], place[1]
    sources = (owners_in, order_in, lon_in, lat_in, offset_in)
    targets = (owners, order, lon, lat, offset)
    small = [
        pltpu.make_async_copy(source, target, small_sems.at[n])
        for n, (source, target) in enumerate(zip(sources, targets))
    ]
    copies = [
        pltpu.make_async_copy(field.at[:, row, :], tile.at[row], sems.at[row])
        for row in range(lon_cells)
    ]
    for copy in small + copies:
        copy.start()
    rows_t[...] = jnp.zeros_like(rows_t)
    lane = lax.broadcasted_iota(jnp.int32, (1, LANES), 1)
    for copy in small + copies:
        copy.wait()

    def gaps(group):
        owner = owners[group]
        return owner // lat_tiles - my_lon, owner % lat_tiles - my_lat

    def near(group):
        lon_gap, lat_gap = gaps(group)
        return (jnp.abs(lon_gap) <= 1) & (jnp.abs(lat_gap) <= 1)

    @pl.loop(0, groups)
    def _(turn):
        group = order[turn]
        lon_gap, lat_gap = gaps(group)

        @pl.when(near(group))
        def _():
            @pl.loop(0, obs)
            def _(k):
                p = lon_gap * lon_cells + lon[group, k]
                q = lat_gap * lat_cells + lat[group, k]
                a = offset[group, 0, k]
                b = offset[group, 1, k]
                inside = (p >= -1) & (p <= lon_cells) & (q >= -1) & (q <= lat_cells)

                @pl.when(inside)
                def _():
                    first = jnp.clip(q - 1, 0, lat_cells - 1) // LANES
                    last = jnp.clip(q + 1, 0, lat_cells - 1) // LANES

                    def share(chunk):
                        gap = (lane + chunk * LANES - q).astype(jnp.float32)
                        lat_hat = jnp.maximum(1.0 - jnp.abs(gap - b), 0.0)
                        start = pl.multiple_of(chunk * LANES, LANES)
                        total = jnp.zeros((members, LANES), jnp.float32)
                        for step in (-1, 0, 1):
                            row = p + step
                            hat = jnp.maximum(1.0 - jnp.abs(step - a), 0.0)
                            hat = jnp.where((row >= 0) & (row < lon_cells), hat, 0.0)
                            row = jnp.clip(row, 0, lon_cells - 1)
                            total = total + tile[row, :, pl.ds(start, LANES)] * (lat_hat * hat)
                        found = jnp.sum(total, axis=1, keepdims=True)
                        rows_t[...] += jnp.where(lane == turn * obs + k, found, 0.0)

                    share(first)

                    @pl.when(last != first)
                    def _():
                        share(last)


def table_kernel(sizes, value_in, error_in, order_in, values, noises, value, error, order, sems):
    groups, obs, members = sizes[:3]
    copies = [
        pltpu.make_async_copy(source, target, sems.at[n])
        for n, (source, target) in enumerate(
            ((value_in, value), (error_in, error), (order_in, order))
        )
    ]
    for copy in copies:
        copy.start()
    for copy in copies:
        copy.wait()
    for turn in range(groups):
        group = order[turn]
        for k in range(obs):
            row = pl.ds(turn * obs + k, 1)
            values[row, :] = jnp.full((1, LANES), value[group, k], jnp.float32)
            noises[row, :] = jnp.full((1, LANES), error[group, k] * (members - 1.0), jnp.float32)


def split(x):
    high = x.astype(jnp.bfloat16)
    return high, (x - high.astype(jnp.float32)).astype(jnp.bfloat16)


def analysis_kernel(
    sizes, rows_t_ref, values, noises, tile, out, done, reduced, spreads, out_sems
):
    groups, obs, members, lon_cells, lat_cells, lat_tiles = sizes
    count = groups * obs
    priors = rows_t_ref[...]
    mean = jnp.mean(priors, axis=0, keepdims=True)
    anomalies = priors - mean
    eye = (
        lax.broadcasted_iota(jnp.int32, (members, LANES), 0)
        == lax.broadcasted_iota(jnp.int32, (members, LANES), 1) % members
    ).astype(jnp.float32)
    both = lax.dot_general(
        anomalies,
        jnp.concatenate([anomalies, eye], axis=1),
        (((0,), (0,)), ((), ())),
        precision=HIGH,
        preferred_element_type=jnp.float32,
    )
    mean_column = jnp.broadcast_to(mean, (LANES, LANES)).T[:count]
    innovation = values[...] - mean_column
    noise = noises[...]
    down = lax.broadcasted_iota(jnp.int32, (count, LANES), 0)
    across = lax.broadcasted_iota(jnp.int32, (count, LANES), 1)
    left_all = both[:count, :LANES] + jnp.where(down == across, noise, 0.0)
    left_all = jnp.where(across == count, innovation, left_all)
    right_all = both[:count, LANES:]

    own = lax.broadcasted_iota(jnp.int32, (obs, LANES), 0)
    half = lax.broadcasted_iota(jnp.int32, (obs, LANES), 1) < members
    for g in range(groups):
        low = g * obs
        tall = 2 * obs if g < groups - 1 else obs
        left = left_all[:tall]
        right = right_all[:tall]
        sub = lax.broadcasted_iota(jnp.int32, (tall, LANES), 0)
        columns = [
            jnp.broadcast_to(left[:, low + i : low + i + 1], (tall, LANES)) for i in range(obs)
        ]
        inverses = jnp.zeros((obs, LANES), jnp.float32)
        shrinks = jnp.zeros((obs, LANES), jnp.float32)
        for j in range(0, obs, 2):
            first, second = columns[j], columns[j + 1]
            corner, cross, other = first[j : j + 1], first[j + 1 : j + 2], second[j + 1 : j + 2]
            inverse = 1.0 / corner
            inverse_next = corner / (corner * other - cross * cross)
            slope = cross * inverse
            shrink = 1.0 / (1.0 + jnp.sqrt(noise[low + j : low + j + 1] * inverse))
            shrink_next = 1.0 / (1.0 + jnp.sqrt(noise[low + j + 1 : low + j + 2] * inverse_next))
            inverses = jnp.where(own == j, inverse, jnp.where(own == j + 1, inverse_next, inverses))
            shrinks = jnp.where(own == j, shrink, jnp.where(own == j + 1, shrink_next, shrinks))
            below = jnp.where(sub > j, first, 0.0)
            below_next = jnp.where(sub > j + 1, second - first * slope, 0.0)

            def eliminate(block, weight, weight_next):
                top, under = block[j : j + 1], block[j + 1 : j + 2]
                scaled = (under - (slope * weight) * top) * (inverse_next * weight_next)
                return block - (below * (top * (inverse * weight)) + below_next * scaled)

            for i in range(j + 2, obs):
                columns[i] = eliminate(columns[i], 1.0, 1.0)
            left = eliminate(left, 1.0, 1.0)
            right = eliminate(
                right, jnp.where(half[0:1], 1.0, shrink), jnp.where(half[0:1], 1.0, shrink_next)
            )
        following = (left[obs:], right[obs:])
        left, right = left[:obs], right[:obs]
        innovations = jnp.broadcast_to(left[:, count : count + 1], (obs, LANES))
        spreads[low : low + obs, :] = inverses * (innovations - shrinks * right)
        right = right * jnp.where(half, 1.0, shrinks)
        reduced[low : low + obs, :] = right
        if g == groups - 2:
            left_all, right_all = following
        elif g < groups - 2:
            change = jnp.dot(
                (left * inverses).T[low + 2 * obs : count],
                jnp.concatenate([left, right], axis=1),
                precision=HIGH,
                preferred_element_type=jnp.float32,
            )
            left_all = jnp.concatenate(
                [following[0], left_all[2 * obs :] - change[:, :LANES]], axis=0
            )
            right_all = jnp.concatenate(
                [following[1], right_all[2 * obs :] - change[:, LANES:]], axis=0
            )

    change = lax.dot_general(
        spreads[...],
        reduced[...],
        (((0,), (0,)), ((), ())),
        precision=HIGH,
        preferred_element_type=jnp.float32,
    )[members : 2 * members, :members]
    high, low_part = split(change)
    weights = jnp.concatenate([high, high, low_part], axis=1)

    @pl.loop(0, lat_cells // LANES)
    def _(c):
        lanes = pl.ds(pl.multiple_of(c * LANES, LANES), LANES)
        for part in range(lon_cells // STEP):
            rows = range(part * STEP, (part + 1) * STEP)
            block = jnp.concatenate([tile[row, :, lanes] for row in rows], axis=1)
            top, rest = split(block)
            new = block + jnp.dot(
                weights,
                jnp.concatenate([top, rest, top], axis=0),
                preferred_element_type=jnp.float32,
            )
            for n, row in enumerate(rows):
                done[c, pl.ds(row, members, stride=lon_cells), :] = new[
                    :, n * LANES : (n + 1) * LANES
                ]
        pltpu.make_async_copy(done.at[c], out.at[:, lanes], out_sems.at[c]).start()

    for c in range(lat_cells // LANES):
        pltpu.make_async_copy(
            done.at[c], out.at[:, pl.ds(c * LANES, LANES)], out_sems.at[c]
        ).wait()


def pairwise_sum(shard, axis, partners):
    size = lax.axis_size(axis)
    arrived = [
        lax.ppermute(shard, axis, [(i, partner(i)) for i in range(size)]) for partner in partners
    ]
    for piece in arrived:
        shard = shard + piece
    return shard


def total_over_tiles(shard):
    quad = (lambda i: i ^ 1, lambda i: i ^ 2, lambda i: i ^ 3)
    shard = pairwise_sum(shard, "lat", (lambda i: i ^ 1,))
    shard = pairwise_sum(shard, "lon_0", quad)
    shard = pairwise_sum(shard, "lon_2", quad)
    shard = pairwise_sum(shard, "lon_1", (lambda i: 7 - i,))
    return pairwise_sum(shard, "lon_1", quad)


def body(ensemble, obs_lon, obs_lat, obs_offset, obs_value, obs_error, owners, group_order):
    members, lon_cells, lat_cells = ensemble.shape
    groups, obs = obs_lon.shape
    sizes = (groups, obs, members, lon_cells, lat_cells, lax.axis_size("lat"))
    count = groups * obs
    place = jnp.stack([lax.axis_index(LON), lax.axis_index("lat")]).astype(jnp.int32)
    smem = pl.BlockSpec(memory_space=pltpu.SMEM)
    vmem = pl.BlockSpec(memory_space=pltpu.VMEM)
    hbm = pl.BlockSpec(memory_space=pltpu.HBM)
    tile_shape = (lon_cells, members, lat_cells)
    field, lon, lat, offset, value, error, owner, order = (
        pltpu.with_memory_space_constraint(array, pltpu.HBM)
        for array in (
            ensemble, obs_lon, obs_lat, obs_offset, obs_value, obs_error, owners, group_order
        )
    )
    rows_t, tile = pl.pallas_call(
        functools.partial(priors_kernel, sizes),
        out_shape=(
            jax.ShapeDtypeStruct((members, LANES), jnp.float32),
            jax.ShapeDtypeStruct(tile_shape, jnp.float32),
        ),
        in_specs=[smem] + [hbm] * 6,
        out_specs=(vmem, vmem),
        scratch_shapes=[
            pltpu.SMEM(obs_lon.shape, jnp.int32),
            pltpu.SMEM(obs_lat.shape, jnp.int32),
            pltpu.SMEM(obs_offset.shape, jnp.float32),
            pltpu.SMEM(owners.shape, jnp.int32),
            pltpu.SMEM(group_order.shape, jnp.int32),
            pltpu.SemaphoreType.DMA((5,)),
            pltpu.SemaphoreType.DMA((lon_cells,)),
        ],
        compiler_params=pltpu.CompilerParams(vmem_limit_bytes=10 << 20),
        name="priors",
    )(place, lon, lat, offset, owner, order, field)
    values, noises = pl.pallas_call(
        functools.partial(table_kernel, sizes),
        out_shape=(jax.ShapeDtypeStruct((count, LANES), jnp.float32),) * 2,
        in_specs=[hbm] * 3,
        out_specs=(vmem, vmem),
        scratch_shapes=[
            pltpu.SMEM(obs_value.shape, jnp.float32),
            pltpu.SMEM(obs_error.shape, jnp.float32),
            pltpu.SMEM(group_order.shape, jnp.int32),
            pltpu.SemaphoreType.DMA((3,)),
        ],
        compiler_params=pltpu.CompilerParams(vmem_limit_bytes=1 << 20),
        cost_estimate=pl.CostEstimate(flops=1 << 20, bytes_accessed=4 << 20, transcendentals=0),
        name="tables",
    )(value, error, order)
    rows_t = total_over_tiles(rows_t)
    return pl.pallas_call(
        functools.partial(analysis_kernel, sizes),
        out_shape=jax.ShapeDtypeStruct((members * lon_cells, lat_cells), jnp.float32),
        in_specs=[vmem] * 4,
        out_specs=hbm,
        scratch_shapes=[
            pltpu.VMEM((lat_cells // LANES, members * lon_cells, LANES), jnp.float32),
            pltpu.VMEM((count, LANES), jnp.float32),
            pltpu.VMEM((count, LANES), jnp.float32),
            pltpu.SemaphoreType.DMA((lat_cells // LANES,)),
        ],
        compiler_params=pltpu.CompilerParams(vmem_limit_bytes=16 << 20),
        name="analysis",
    )(rows_t, values, noises, tile).reshape(ensemble.shape)


def solution(mesh):
    torus = Mesh(
        mesh.devices.reshape(4, 8, 4, mesh.shape["lat"]), ("lon_0", "lon_1", "lon_2", "lat")
    )
    in_specs = (P(None, LON, "lat"), P(), P(), P(), P(), P(), P(), P())
    out_specs = P(None, LON, "lat")
    return jax.shard_map(body, mesh=torus, in_specs=in_specs, out_specs=out_specs, check_vma=False)
```

```python
import functools

import jax
import jax.numpy as jnp
from jax import lax
from jax.experimental import pallas as pl
from jax.experimental.pallas import tpu as pltpu
from jax.sharding import Mesh
from jax.sharding import PartitionSpec as P

LON = ("lon_0", "lon_1", "lon_2")
LANES = 128
STEP = 4
HIGH = lax.Precision.HIGHEST


def priors_kernel(
    sizes, lon_in, lat_in, offset_in, owners_in, order_in, field,
    rows_t, tile, lon, lat, offset, owners, order, small_sems, sems
):
    groups, obs, members, lon_cells, lat_cells, lat_tiles = sizes
    my_lon, my_lat = lax.axis_index(LON), lax.axis_index("lat")
    sources = (owners_in, order_in, lon_in, lat_in, offset_in)
    targets = (owners, order, lon, lat, offset)
    small = [
        pltpu.make_async_copy(source, target, small_sems.at[n])
        for n, (source, target) in enumerate(zip(sources, targets))
    ]
    copies = [
        pltpu.make_async_copy(field.at[:, row, :], tile.at[row], sems.at[row])
        for row in range(lon_cells)
    ]
    for copy in small + copies:
        copy.start()
    rows_t[...] = jnp.zeros_like(rows_t)
    lane = lax.broadcasted_iota(jnp.int32, (1, LANES), 1)
    for copy in small + copies:
        copy.wait()

    def gaps(group):
        owner = owners[group]
        return owner // lat_tiles - my_lon, owner % lat_tiles - my_lat

    def near(group):
        lon_gap, lat_gap = gaps(group)
        return (jnp.abs(lon_gap) <= 1) & (jnp.abs(lat_gap) <= 1)

    @pl.loop(0, groups)
    def _(turn):
        group = order[turn]
        lon_gap, lat_gap = gaps(group)

        @pl.when(near(group))
        def _():
            @pl.loop(0, obs)
            def _(k):
                p = lon_gap * lon_cells + lon[group, k]
                q = lat_gap * lat_cells + lat[group, k]
                a = offset[group, 0, k]
                b = offset[group, 1, k]
                inside = (p >= -1) & (p <= lon_cells) & (q >= -1) & (q <= lat_cells)

                @pl.when(inside)
                def _():
                    first = jnp.clip(q - 1, 0, lat_cells - 1) // LANES
                    last = jnp.clip(q + 1, 0, lat_cells - 1) // LANES

                    def share(chunk):
                        gap = (lane + chunk * LANES - q).astype(jnp.float32)
                        lat_hat = jnp.maximum(1.0 - jnp.abs(gap - b), 0.0)
                        start = pl.multiple_of(chunk * LANES, LANES)
                        total = jnp.zeros((members, LANES), jnp.float32)
                        for step in (-1, 0, 1):
                            row = p + step
                            hat = jnp.maximum(1.0 - jnp.abs(step - a), 0.0)
                            hat = jnp.where((row >= 0) & (row < lon_cells), hat, 0.0)
                            row = jnp.clip(row, 0, lon_cells - 1)
                            total = total + tile[row, :, pl.ds(start, LANES)] * (lat_hat * hat)
                        found = jnp.sum(total, axis=1, keepdims=True)
                        rows_t[...] += jnp.where(lane == turn * obs + k, found, 0.0)

                    share(first)

                    @pl.when(last != first)
                    def _():
                        share(last)


def table_kernel(sizes, value_in, error_in, order_in, values, noises, value, error, order, sems):
    groups, obs, members = sizes[:3]
    copies = [
        pltpu.make_async_copy(source, target, sems.at[n])
        for n, (source, target) in enumerate(
            ((value_in, value), (error_in, error), (order_in, order))
        )
    ]
    for copy in copies:
        copy.start()
    for copy in copies:
        copy.wait()
    for turn in range(groups):
        group = order[turn]
        for k in range(obs):
            row = pl.ds(turn * obs + k, 1)
            values[row, :] = jnp.full((1, LANES), value[group, k], jnp.float32)
            noises[row, :] = jnp.full((1, LANES), error[group, k] * (members - 1.0), jnp.float32)


def split(x):
    high = x.astype(jnp.bfloat16)
    return high, (x - high.astype(jnp.float32)).astype(jnp.bfloat16)


def analysis_kernel(
    sizes, rows_t_ref, values, noises, tile, out, done, reduced, spreads, out_sems
):
    groups, obs, members, lon_cells, lat_cells, lat_tiles = sizes
    count = groups * obs
    priors = rows_t_ref[...]
    mean = jnp.mean(priors, axis=0, keepdims=True)
    anomalies = priors - mean
    eye = (
        lax.broadcasted_iota(jnp.int32, (members, LANES), 0)
        == lax.broadcasted_iota(jnp.int32, (members, LANES), 1) % members
    ).astype(jnp.float32)
    both = lax.dot_general(
        anomalies,
        jnp.concatenate([anomalies, eye], axis=1),
        (((0,), (0,)), ((), ())),
        precision=HIGH,
        preferred_element_type=jnp.float32,
    )
    mean_column = jnp.broadcast_to(mean, (LANES, LANES)).T[:count]
    innovation = values[...] - mean_column
    noise = noises[...]
    down = lax.broadcasted_iota(jnp.int32, (count, LANES), 0)
    across = lax.broadcasted_iota(jnp.int32, (count, LANES), 1)
    left_all = both[:count, :LANES] + jnp.where(down == across, noise, 0.0)
    left_all = jnp.where(across == count, innovation, left_all)
    right_all = both[:count, LANES:]

    own = lax.broadcasted_iota(jnp.int32, (obs, LANES), 0)
    half = lax.broadcasted_iota(jnp.int32, (obs, LANES), 1) < members
    for g in range(groups):
        low = g * obs
        tall = 2 * obs if g < groups - 1 else obs
        left = left_all[:tall]
        right = right_all[:tall]
        sub = lax.broadcasted_iota(jnp.int32, (tall, LANES), 0)
        columns = [
            jnp.broadcast_to(left[:, low + i : low + i + 1], (tall, LANES)) for i in range(obs)
        ]
        inverses = jnp.zeros((obs, LANES), jnp.float32)
        shrinks = jnp.zeros((obs, LANES), jnp.float32)
        for j in range(0, obs, 2):
            first, second = columns[j], columns[j + 1]
            corner, cross, other = first[j : j + 1], first[j + 1 : j + 2], second[j + 1 : j + 2]
            inverse = 1.0 / corner
            inverse_next = corner / (corner * other - cross * cross)
            slope = cross * inverse
            shrink = 1.0 / (1.0 + jnp.sqrt(noise[low + j : low + j + 1] * inverse))
            shrink_next = 1.0 / (1.0 + jnp.sqrt(noise[low + j + 1 : low + j + 2] * inverse_next))
            inverses = jnp.where(own == j, inverse, jnp.where(own == j + 1, inverse_next, inverses))
            shrinks = jnp.where(own == j, shrink, jnp.where(own == j + 1, shrink_next, shrinks))
            below = jnp.where(sub > j, first, 0.0)
            below_next = jnp.where(sub > j + 1, second - first * slope, 0.0)

            def eliminate(block, weight, weight_next):
                top, under = block[j : j + 1], block[j + 1 : j + 2]
                scaled = (under - (slope * weight) * top) * (inverse_next * weight_next)
                return block - (below * (top * (inverse * weight)) + below_next * scaled)

            for i in range(j + 2, obs):
                columns[i] = eliminate(columns[i], 1.0, 1.0)
            left = eliminate(left, 1.0, 1.0)
            right = eliminate(
                right, jnp.where(half[0:1], 1.0, shrink), jnp.where(half[0:1], 1.0, shrink_next)
            )
        following = (left[obs:], right[obs:])
        left, right = left[:obs], right[:obs]
        innovations = jnp.broadcast_to(left[:, count : count + 1], (obs, LANES))
        spreads[low : low + obs, :] = inverses * (innovations - shrinks * right)
        right = right * jnp.where(half, 1.0, shrinks)
        reduced[low : low + obs, :] = right
        if g == groups - 2:
            left_all, right_all = following
        elif g < groups - 2:
            change = jnp.dot(
                (left * inverses).T[low + 2 * obs : count],
                jnp.concatenate([left, right], axis=1),
                precision=HIGH,
                preferred_element_type=jnp.float32,
            )
            left_all = jnp.concatenate(
                [following[0], left_all[2 * obs :] - change[:, :LANES]], axis=0
            )
            right_all = jnp.concatenate(
                [following[1], right_all[2 * obs :] - change[:, LANES:]], axis=0
            )

    change = lax.dot_general(
        spreads[...],
        reduced[...],
        (((0,), (0,)), ((), ())),
        precision=HIGH,
        preferred_element_type=jnp.float32,
    )[members : 2 * members, :members]
    high, low_part = split(change)
    weights = jnp.concatenate([high, high, low_part], axis=1)

    @pl.loop(0, lat_cells // LANES)
    def _(c):
        lanes = pl.ds(pl.multiple_of(c * LANES, LANES), LANES)
        for part in range(lon_cells // STEP):
            rows = range(part * STEP, (part + 1) * STEP)
            block = jnp.concatenate([tile[row, :, lanes] for row in rows], axis=1)
            top, rest = split(block)
            new = block + jnp.dot(
                weights,
                jnp.concatenate([top, rest, top], axis=0),
                preferred_element_type=jnp.float32,
            )
            for n, row in enumerate(rows):
                done[c, pl.ds(row, members, stride=lon_cells), :] = new[
                    :, n * LANES : (n + 1) * LANES
                ]
        pltpu.make_async_copy(done.at[c], out.at[:, lanes], out_sems.at[c]).start()

    for c in range(lat_cells // LANES):
        pltpu.make_async_copy(
            done.at[c], out.at[:, pl.ds(c * LANES, LANES)], out_sems.at[c]
        ).wait()


def pairwise_sum(shard, axis, partners):
    size = lax.axis_size(axis)
    arrived = [
        lax.ppermute(shard, axis, [(i, partner(i)) for i in range(size)]) for partner in partners
    ]
    for piece in arrived:
        shard = shard + piece
    return shard


def total_over_tiles(shard):
    quad = (lambda i: i ^ 1, lambda i: i ^ 2, lambda i: i ^ 3)
    shard = pairwise_sum(shard, "lat", (lambda i: i ^ 1,))
    shard = pairwise_sum(shard, "lon_0", quad)
    shard = pairwise_sum(shard, "lon_2", quad)
    shard = pairwise_sum(shard, "lon_1", (lambda i: 7 - i,))
    return pairwise_sum(shard, "lon_1", quad)


def body(ensemble, obs_lon, obs_lat, obs_offset, obs_value, obs_error, owners, group_order):
    members, lon_cells, lat_cells = ensemble.shape
    groups, obs = obs_lon.shape
    sizes = (groups, obs, members, lon_cells, lat_cells, lax.axis_size("lat"))
    count = groups * obs
    vmem = pl.BlockSpec(memory_space=pltpu.VMEM)
    hbm = pl.BlockSpec(memory_space=pltpu.HBM)
    tile_shape = (lon_cells, members, lat_cells)
    field, lon, lat, offset, value, error, owner, order = (
        pltpu.with_memory_space_constraint(array, pltpu.HBM)
        for array in (
            ensemble, obs_lon, obs_lat, obs_offset, obs_value, obs_error, owners, group_order
        )
    )
    rows_t, tile = pl.pallas_call(
        functools.partial(priors_kernel, sizes),
        out_shape=(
            jax.ShapeDtypeStruct((members, LANES), jnp.float32),
            jax.ShapeDtypeStruct(tile_shape, jnp.float32),
        ),
        in_specs=[hbm] * 6,
        out_specs=(vmem, vmem),
        scratch_shapes=[
            pltpu.SMEM(obs_lon.shape, jnp.int32),
            pltpu.SMEM(obs_lat.shape, jnp.int32),
            pltpu.SMEM(obs_offset.shape, jnp.float32),
            pltpu.SMEM(owners.shape, jnp.int32),
            pltpu.SMEM(group_order.shape, jnp.int32),
            pltpu.SemaphoreType.DMA((5,)),
            pltpu.SemaphoreType.DMA((lon_cells,)),
        ],
        compiler_params=pltpu.CompilerParams(vmem_limit_bytes=10 << 20),
        name="priors",
    )(lon, lat, offset, owner, order, field)
    values, noises = pl.pallas_call(
        functools.partial(table_kernel, sizes),
        out_shape=(jax.ShapeDtypeStruct((count, LANES), jnp.float32),) * 2,
        in_specs=[hbm] * 3,
        out_specs=(vmem, vmem),
        scratch_shapes=[
            pltpu.SMEM(obs_value.shape, jnp.float32),
            pltpu.SMEM(obs_error.shape, jnp.float32),
            pltpu.SMEM(group_order.shape, jnp.int32),
            pltpu.SemaphoreType.DMA((3,)),
        ],
        compiler_params=pltpu.CompilerParams(vmem_limit_bytes=1 << 20),
        cost_estimate=pl.CostEstimate(flops=1 << 20, bytes_accessed=4 << 20, transcendentals=0),
        name="tables",
    )(value, error, order)
    rows_t = total_over_tiles(rows_t)
    return pl.pallas_call(
        functools.partial(analysis_kernel, sizes),
        out_shape=jax.ShapeDtypeStruct((members * lon_cells, lat_cells), jnp.float32),
        in_specs=[vmem] * 4,
        out_specs=hbm,
        scratch_shapes=[
            pltpu.VMEM((lat_cells // LANES, members * lon_cells, LANES), jnp.float32),
            pltpu.VMEM((count, LANES), jnp.float32),
            pltpu.VMEM((count, LANES), jnp.float32),
            pltpu.SemaphoreType.DMA((lat_cells // LANES,)),
        ],
        compiler_params=pltpu.CompilerParams(vmem_limit_bytes=16 << 20),
        name="analysis",
    )(rows_t, values, noises, tile).reshape(ensemble.shape)


def solution(mesh):
    torus = Mesh(
        mesh.devices.reshape(4, 8, 4, mesh.shape["lat"]), ("lon_0", "lon_1", "lon_2", "lat")
    )
    in_specs = (P(None, LON, "lat"), P(), P(), P(), P(), P(), P(), P())
    out_specs = P(None, LON, "lat")
    return jax.shard_map(body, mesh=torus, in_specs=in_specs, out_specs=out_specs, check_vma=False)
```

```python
import functools

import jax
import jax.numpy as jnp
from jax import lax
from jax.experimental import pallas as pl
from jax.experimental.pallas import tpu as pltpu
from jax.sharding import Mesh
from jax.sharding import PartitionSpec as P

LON = ("lon_0", "lon_1", "lon_2")
LANES = 128
STEP = 4
HIGH = lax.Precision.HIGHEST


def priors_kernel(
    sizes, lon_in, lat_in, offset_in, owners_in, order_in, field,
    rows_t, tile, lon, lat, offset, owners, order, small_sems, sems
):
    groups, obs, members, lon_cells, lat_cells, lat_tiles = sizes
    my_lon, my_lat = lax.axis_index(LON), lax.axis_index("lat")
    sources = (owners_in, order_in, lon_in, lat_in, offset_in)
    targets = (owners, order, lon, lat, offset)
    small = [
        pltpu.make_async_copy(source, target, small_sems.at[n])
        for n, (source, target) in enumerate(zip(sources, targets))
    ]
    copies = [
        pltpu.make_async_copy(field.at[:, row, :], tile.at[row], sems.at[row])
        for row in range(lon_cells)
    ]
    for copy in small + copies:
        copy.start()
    rows_t[...] = jnp.zeros_like(rows_t)
    lane = lax.broadcasted_iota(jnp.int32, (1, LANES), 1)
    for copy in small + copies:
        copy.wait()

    def gaps(group):
        owner = owners[group]
        return owner // lat_tiles - my_lon, owner % lat_tiles - my_lat

    def near(group):
        lon_gap, lat_gap = gaps(group)
        return (jnp.abs(lon_gap) <= 1) & (jnp.abs(lat_gap) <= 1)

    @pl.loop(0, groups)
    def _(turn):
        group = order[turn]
        lon_gap, lat_gap = gaps(group)

        @pl.when(near(group))
        def _():
            @pl.loop(0, obs)
            def _(k):
                p = lon_gap * lon_cells + lon[group, k]
                q = lat_gap * lat_cells + lat[group, k]
                a = offset[group, 0, k]
                b = offset[group, 1, k]
                inside = (p >= -1) & (p <= lon_cells) & (q >= -1) & (q <= lat_cells)

                @pl.when(inside)
                def _():
                    first = jnp.clip(q - 1, 0, lat_cells - 1) // LANES
                    last = jnp.clip(q + 1, 0, lat_cells - 1) // LANES

                    def share(chunk):
                        gap = (lane + chunk * LANES - q).astype(jnp.float32)
                        lat_hat = jnp.maximum(1.0 - jnp.abs(gap - b), 0.0)
                        start = pl.multiple_of(chunk * LANES, LANES)
                        total = jnp.zeros((members, LANES), jnp.float32)
                        for step in (-1, 0, 1):
                            row = p + step
                            hat = jnp.maximum(1.0 - jnp.abs(step - a), 0.0)
                            hat = jnp.where((row >= 0) & (row < lon_cells), hat, 0.0)
                            row = jnp.clip(row, 0, lon_cells - 1)
                            total = total + tile[row, :, pl.ds(start, LANES)] * (lat_hat * hat)
                        found = jnp.sum(total, axis=1, keepdims=True)
                        index = turn * obs + k
                        wide = jnp.where(index < 64, index, 1000)
                        narrow = jnp.where(index < 64, -1000, index - 64)
                        rows_t[0:32, :] += jnp.where(lane == wide, found[0:32], 0.0) + jnp.where(
                            lane == wide + 64, found[32:64], 0.0
                        )
                        tail = jnp.zeros((16, LANES), jnp.float32)
                        for q4 in range(4):
                            piece = found[q4 * 16 : q4 * 16 + 16]
                            tail = jnp.where(lane == narrow + q4 * 32, piece, tail)
                        rows_t[32:48, :] += tail

                    share(first)

                    @pl.when(last != first)
                    def _():
                        share(last)


def table_kernel(sizes, value_in, error_in, order_in, values, noises, value, error, order, sems):
    groups, obs, members = sizes[:3]
    copies = [
        pltpu.make_async_copy(source, target, sems.at[n])
        for n, (source, target) in enumerate(
            ((value_in, value), (error_in, error), (order_in, order))
        )
    ]
    for copy in copies:
        copy.start()
    for copy in copies:
        copy.wait()
    for turn in range(groups):
        group = order[turn]
        for k in range(obs):
            row = pl.ds(turn * obs + k, 1)
            values[row, :] = jnp.full((1, LANES), value[group, k], jnp.float32)
            noises[row, :] = jnp.full((1, LANES), error[group, k] * (members - 1.0), jnp.float32)


def split(x):
    high = x.astype(jnp.bfloat16)
    return high, (x - high.astype(jnp.float32)).astype(jnp.bfloat16)


def analysis_kernel(
    sizes, rows_t_ref, values, noises, tile, out, done, reduced, spreads, out_sems
):
    groups, obs, members, lon_cells, lat_cells, lat_tiles = sizes
    count = groups * obs
    packed = rows_t_ref[0:32, :]
    early = jnp.concatenate([packed, pltpu.roll(packed, 64, 1)], axis=0)
    tail = rows_t_ref[32:48, :]
    late = jnp.concatenate(
        [tail if n == 2 else pltpu.roll(tail, (64 - 32 * n) % LANES, 1) for n in range(4)], axis=0
    )
    at = lax.broadcasted_iota(jnp.int32, (members, LANES), 1)
    priors = jnp.where(at < 64, early, jnp.where(at < groups * obs, late, 0.0))
    mean = jnp.mean(priors, axis=0, keepdims=True)
    anomalies = priors - mean
    eye = (
        lax.broadcasted_iota(jnp.int32, (members, LANES), 0)
        == lax.broadcasted_iota(jnp.int32, (members, LANES), 1) % members
    ).astype(jnp.float32)
    both = lax.dot_general(
        anomalies,
        jnp.concatenate([anomalies, eye], axis=1),
        (((0,), (0,)), ((), ())),
        precision=HIGH,
        preferred_element_type=jnp.float32,
    )
    mean_column = jnp.broadcast_to(mean, (LANES, LANES)).T[:count]
    innovation = values[...] - mean_column
    noise = noises[...]
    down = lax.broadcasted_iota(jnp.int32, (count, LANES), 0)
    across = lax.broadcasted_iota(jnp.int32, (count, LANES), 1)
    left_all = both[:count, :LANES] + jnp.where(down == across, noise, 0.0)
    left_all = jnp.where(across == count, innovation, left_all)
    right_all = both[:count, LANES:]

    own = lax.broadcasted_iota(jnp.int32, (obs, LANES), 0)
    half = lax.broadcasted_iota(jnp.int32, (obs, LANES), 1) < members
    for g in range(groups):
        low = g * obs
        tall = 2 * obs if g < groups - 1 else obs
        left = left_all[:tall]
        right = right_all[:tall]
        sub = lax.broadcasted_iota(jnp.int32, (tall, LANES), 0)
        columns = [
            jnp.broadcast_to(left[:, low + i : low + i + 1], (tall, LANES)) for i in range(obs)
        ]
        inverses = jnp.zeros((obs, LANES), jnp.float32)
        shrinks = jnp.zeros((obs, LANES), jnp.float32)
        for j in range(0, obs, 2):
            first, second = columns[j], columns[j + 1]
            corner, cross, other = first[j : j + 1], first[j + 1 : j + 2], second[j + 1 : j + 2]
            inverse = 1.0 / corner
            inverse_next = corner / (corner * other - cross * cross)
            slope = cross * inverse
            shrink = 1.0 / (1.0 + jnp.sqrt(noise[low + j : low + j + 1] * inverse))
            shrink_next = 1.0 / (1.0 + jnp.sqrt(noise[low + j + 1 : low + j + 2] * inverse_next))
            inverses = jnp.where(own == j, inverse, jnp.where(own == j + 1, inverse_next, inverses))
            shrinks = jnp.where(own == j, shrink, jnp.where(own == j + 1, shrink_next, shrinks))
            below = jnp.where(sub > j, first, 0.0)
            below_next = jnp.where(sub > j + 1, second - first * slope, 0.0)

            def eliminate(block, weight, weight_next):
                top, under = block[j : j + 1], block[j + 1 : j + 2]
                scaled = (under - (slope * weight) * top) * (inverse_next * weight_next)
                return block - (below * (top * (inverse * weight)) + below_next * scaled)

            for i in range(j + 2, obs):
                columns[i] = eliminate(columns[i], 1.0, 1.0)
            left = eliminate(left, 1.0, 1.0)
            right = eliminate(
                right, jnp.where(half[0:1], 1.0, shrink), jnp.where(half[0:1], 1.0, shrink_next)
            )
        following = (left[obs:], right[obs:])
        left, right = left[:obs], right[:obs]
        innovations = jnp.broadcast_to(left[:, count : count + 1], (obs, LANES))
        spreads[low : low + obs, :] = inverses * (innovations - shrinks * right)
        right = right * jnp.where(half, 1.0, shrinks)
        reduced[low : low + obs, :] = right
        if g == groups - 2:
            left_all, right_all = following
        elif g < groups - 2:
            change = jnp.dot(
                (left * inverses).T[low + 2 * obs : count],
                jnp.concatenate([left, right], axis=1),
                precision=HIGH,
                preferred_element_type=jnp.float32,
            )
            left_all = jnp.concatenate(
                [following[0], left_all[2 * obs :] - change[:, :LANES]], axis=0
            )
            right_all = jnp.concatenate(
                [following[1], right_all[2 * obs :] - change[:, LANES:]], axis=0
            )

    change = lax.dot_general(
        spreads[...],
        reduced[...],
        (((0,), (0,)), ((), ())),
        precision=HIGH,
        preferred_element_type=jnp.float32,
    )[members : 2 * members, :members]
    high, low_part = split(change)
    weights = jnp.concatenate([high, high, low_part], axis=1)

    @pl.loop(0, lat_cells // LANES)
    def _(c):
        lanes = pl.ds(pl.multiple_of(c * LANES, LANES), LANES)
        for part in range(lon_cells // STEP):
            rows = range(part * STEP, (part + 1) * STEP)
            block = jnp.concatenate([tile[row, :, lanes] for row in rows], axis=1)
            top, rest = split(block)
            new = block + jnp.dot(
                weights,
                jnp.concatenate([top, rest, top], axis=0),
                preferred_element_type=jnp.float32,
            )
            for n, row in enumerate(rows):
                done[c, pl.ds(row, members, stride=lon_cells), :] = new[
                    :, n * LANES : (n + 1) * LANES
                ]
        pltpu.make_async_copy(done.at[c], out.at[:, lanes], out_sems.at[c]).start()

    for c in range(lat_cells // LANES):
        pltpu.make_async_copy(
            done.at[c], out.at[:, pl.ds(c * LANES, LANES)], out_sems.at[c]
        ).wait()


def pairwise_sum(shard, axis, partners):
    size = lax.axis_size(axis)
    arrived = [
        lax.ppermute(shard, axis, [(i, partner(i)) for i in range(size)]) for partner in partners
    ]
    for piece in arrived:
        shard = shard + piece
    return shard


def total_over_tiles(shard):
    quad = (lambda i: i ^ 1, lambda i: i ^ 2, lambda i: i ^ 3)
    shard = pairwise_sum(shard, "lat", (lambda i: i ^ 1,))
    shard = pairwise_sum(shard, "lon_0", quad)
    shard = pairwise_sum(shard, "lon_2", quad)
    shard = pairwise_sum(shard, "lon_1", (lambda i: 7 - i,))
    return pairwise_sum(shard, "lon_1", quad)


def body(ensemble, obs_lon, obs_lat, obs_offset, obs_value, obs_error, owners, group_order):
    members, lon_cells, lat_cells = ensemble.shape
    groups, obs = obs_lon.shape
    sizes = (groups, obs, members, lon_cells, lat_cells, lax.axis_size("lat"))
    count = groups * obs
    vmem = pl.BlockSpec(memory_space=pltpu.VMEM)
    hbm = pl.BlockSpec(memory_space=pltpu.HBM)
    tile_shape = (lon_cells, members, lat_cells)
    field, lon, lat, offset, value, error, owner, order = (
        pltpu.with_memory_space_constraint(array, pltpu.HBM)
        for array in (
            ensemble, obs_lon, obs_lat, obs_offset, obs_value, obs_error, owners, group_order
        )
    )
    rows_t, tile = pl.pallas_call(
        functools.partial(priors_kernel, sizes),
        out_shape=(
            jax.ShapeDtypeStruct((count * members // LANES, LANES), jnp.float32),
            jax.ShapeDtypeStruct(tile_shape, jnp.float32),
        ),
        in_specs=[hbm] * 6,
        out_specs=(vmem, vmem),
        scratch_shapes=[
            pltpu.SMEM(obs_lon.shape, jnp.int32),
            pltpu.SMEM(obs_lat.shape, jnp.int32),
            pltpu.SMEM(obs_offset.shape, jnp.float32),
            pltpu.SMEM(owners.shape, jnp.int32),
            pltpu.SMEM(group_order.shape, jnp.int32),
            pltpu.SemaphoreType.DMA((5,)),
            pltpu.SemaphoreType.DMA((lon_cells,)),
        ],
        compiler_params=pltpu.CompilerParams(vmem_limit_bytes=10 << 20),
        name="priors",
    )(lon, lat, offset, owner, order, field)
    values, noises = pl.pallas_call(
        functools.partial(table_kernel, sizes),
        out_shape=(jax.ShapeDtypeStruct((count, LANES), jnp.float32),) * 2,
        in_specs=[hbm] * 3,
        out_specs=(vmem, vmem),
        scratch_shapes=[
            pltpu.SMEM(obs_value.shape, jnp.float32),
            pltpu.SMEM(obs_error.shape, jnp.float32),
            pltpu.SMEM(group_order.shape, jnp.int32),
            pltpu.SemaphoreType.DMA((3,)),
        ],
        compiler_params=pltpu.CompilerParams(vmem_limit_bytes=1 << 20),
        cost_estimate=pl.CostEstimate(flops=1 << 20, bytes_accessed=4 << 20, transcendentals=0),
        name="tables",
    )(value, error, order)
    rows_t = total_over_tiles(rows_t)
    return pl.pallas_call(
        functools.partial(analysis_kernel, sizes),
        out_shape=jax.ShapeDtypeStruct((members * lon_cells, lat_cells), jnp.float32),
        in_specs=[vmem] * 4,
        out_specs=hbm,
        scratch_shapes=[
            pltpu.VMEM((lat_cells // LANES, members * lon_cells, LANES), jnp.float32),
            pltpu.VMEM((count, LANES), jnp.float32),
            pltpu.VMEM((count, LANES), jnp.float32),
            pltpu.SemaphoreType.DMA((lat_cells // LANES,)),
        ],
        compiler_params=pltpu.CompilerParams(vmem_limit_bytes=16 << 20),
        name="analysis",
    )(rows_t, values, noises, tile).reshape(ensemble.shape)


def solution(mesh):
    torus = Mesh(
        mesh.devices.reshape(4, 8, 4, mesh.shape["lat"]), ("lon_0", "lon_1", "lon_2", "lat")
    )
    in_specs = (P(None, LON, "lat"), P(), P(), P(), P(), P(), P(), P())
    out_specs = P(None, LON, "lat")
    return jax.shard_map(body, mesh=torus, in_specs=in_specs, out_specs=out_specs, check_vma=False)
```
